32 devices in a mesh: grp: 8 (over y, x, core), leaf: 4 (over z).
Axes of the slice: x: 2, y: 2, z: 4, core: 2. Of those that a mesh axis runs over, the one named last changes fastest.
Arguments:
- labels: int32 [16384], P(('grp', 'leaf')), may hold values from 0 to 255
- leaf_inverse: float32 [16384, 512], P(('grp', 'leaf')), may hold values from -1 to 4
- leaf_basis: float32 [16384, 128], P(('grp', 'leaf')), may hold values from -0.25 to 0.25
- leaf_solved: float32 [16384, 128], P(('grp', 'leaf')), may hold values from -0.5 to 0.5
- group_capacitance: float32 [4096, 512], P(('grp', 'leaf')), may hold values from -1 to 4
- top_basis: float32 [16384, 128], P(('grp', 'leaf')), may hold values from -0.125 to 0.125
- top_solved: float32 [16384, 128], P(('grp', 'leaf')), may hold values from -0.5 to 0.5
- top_capacitance: float32 [1024, 1024], P('grp'), may hold values from -1 to 4
Outputs:
- dual_box: float32 [16384, 256], P(('grp', 'leaf'))
- scaled_dual: float32 [16384, 256], P(('grp', 'leaf'))
The draws below stay inside these ranges and needn't reach their ends.
All inputs are finite; a program needn't handle non-finite values.
Results may differ from the reference program's by a relative error of at most 0.0003.
Values sent between devices are 32-bit elements; how exact they have to be, the bound alone decides.
A program may use at most 64 MiB of HBM per device.

```python
import math
import jax
import jax.numpy as jnp
from jax import lax

LEAF = 512
RANK = 128
CLASSES = 256
ITERS = 2
CAP = 512
TOPCAP = 1024
ROWS = 16384
N_GRP = 8
N_LEAF = 4


def dominant(key, height, order):
    first, second = jax.random.split(key, 2)
    noise = jnp.clip(jax.random.normal(first, (height, order), jnp.float32), -4.0, 4.0) * 0.4
    noise = noise / math.sqrt(order)
    diagonal = jax.random.uniform(second, (height, 1), jnp.float32, 0.5, 1.5)
    position = lax.broadcasted_iota(jnp.int32, (height, order), 0) % order
    column = lax.broadcasted_iota(jnp.int32, (height, order), 1)
    identity = (position == column).astype(jnp.float32)
    return identity * diagonal + noise


def draw_leaf_inverse(key, part):
    return dominant(jax.random.fold_in(key, 11), ROWS, LEAF)


def draw_group_capacitance(key, part):
    return dominant(jax.random.fold_in(key, 23), N_GRP * CAP, CAP)


def draw_top_capacitance(key, part):
    return dominant(jax.random.fold_in(key, 37), TOPCAP, TOPCAP)


def place_ends(array, own_key, smallest, top_value):
    shape = array.shape
    place = [jax.random.randint(jax.random.fold_in(own_key, axis), (), 0, shape[axis]) for axis in range(len(shape))]
    array = array.at[tuple(place)].set(smallest)
    longest = shape.index(max(shape))
    place[longest] = (place[longest] + 1) % shape[longest]
    return array.at[tuple(place)].set(top_value)


def block_scale(rng, shape, cuts, low, top_value):
    def one(axis_at, shards_of):
        draws = jax.random.uniform(jax.random.fold_in(jax.random.fold_in(rng, 6), axis_at), (shards_of,), jnp.float32, low / len(cuts), top_value / len(cuts))
        return jnp.repeat(jnp.exp(draws), shape[axis_at] // shards_of).reshape((-1,) + (1,) * (len(shape) - axis_at - 1))

    factor_of = one(*cuts[0])
    for cut in cuts[1:]:
        factor_of = factor_of * one(*cut)
    return factor_of


def normal_values(key, shape, scale, most, cuts=(), dtype=jnp.bfloat16):
    factor_of = block_scale(key, shape, cuts, -0.22, 0.18) if cuts else 1.0
    result = jax.random.normal(key, shape, jnp.float32) * scale * factor_of
    return jnp.minimum(jnp.maximum(result, -most), most).astype(dtype)


def setup_inputs(seed: int = 0) -> dict:
    keys = jax.random.split(jax.random.key(seed), 9)
    return {
        "labels": place_ends(jax.random.randint(keys[0], (ROWS,), 0, CLASSES), jax.random.fold_in(keys[0], 1), 0, CLASSES - 1).astype(jnp.int32),
        "leaf_inverse": draw_leaf_inverse(jax.random.fold_in(keys[8], 71), 0),
        "leaf_basis": normal_values(keys[2], (ROWS, RANK), LEAF ** -0.5, 0.25, ((0, 32),), jnp.float32),
        "leaf_solved": normal_values(keys[3], (ROWS, RANK), RANK ** -0.5, 0.5, ((0, 32),), jnp.float32),
        "group_capacitance": draw_group_capacitance(jax.random.fold_in(keys[8], 71), 0),
        "top_basis": normal_values(keys[5], (ROWS, RANK), (LEAF * N_LEAF) ** -0.5, 0.125, ((0, 32),), jnp.float32),
        "top_solved": normal_values(keys[6], (ROWS, RANK), RANK ** -0.5, 0.5, ((0, 32),), jnp.float32),
        "top_capacitance": draw_top_capacitance(jax.random.fold_in(keys[8], 71), 0),
    }


high = lax.Precision.HIGHEST


def reference(labels, leaf_inverse, leaf_basis, leaf_solved, group_capacitance, top_basis, top_solved, top_capacitance):
    leaves = N_GRP * N_LEAF
    columns = lax.broadcasted_iota(jnp.int32, (ROWS, CLASSES), 1)
    label_sign = jnp.where(labels[:, None] == columns, 1.0, -1.0).astype(jnp.float32)
    blocks = leaf_inverse.reshape(leaves, LEAF, LEAF)
    basis = leaf_basis.reshape(leaves, LEAF, RANK)
    solved_basis = leaf_solved.reshape(leaves, LEAF, RANK)
    group_blocks = group_capacitance.reshape(N_GRP, CAP, CAP)
    top_rows = top_basis.reshape(leaves, LEAF, RANK)
    top_lift = top_solved.reshape(N_GRP, N_LEAF, LEAF, RANK)
    dual_box = jnp.zeros((ROWS, CLASSES), jnp.float32)
    scaled_dual = jnp.zeros((ROWS, CLASSES), jnp.float32)
    for iteration in range(ITERS):
        rhs = label_sign * (1.0 + 1.0 * (dual_box - scaled_dual))
        local = jnp.einsum("nij,njc->nic", blocks, rhs.reshape(leaves, LEAF, CLASSES), precision=high)
        coeffs = jnp.einsum("nir,nic->nrc", basis, local, precision=high).reshape(N_GRP, CAP, CLASSES)
        group_coef = jnp.einsum("gij,gjc->gic", group_blocks, coeffs, precision=high).reshape(leaves, RANK, CLASSES)
        inner = local - jnp.einsum("nir,nrc->nic", solved_basis, group_coef, precision=high)
        projection = jnp.einsum("nir,nic->nrc", top_rows, inner, precision=high)
        projection = projection.reshape(N_GRP, N_LEAF, RANK, CLASSES).sum(axis=1).reshape(TOPCAP, CLASSES)
        top_coef = jnp.dot(top_capacitance, projection, precision=high).reshape(N_GRP, RANK, CLASSES)
        solved = inner.reshape(N_GRP, N_LEAF, LEAF, CLASSES) - jnp.einsum("glir,grc->glic", top_lift, top_coef, precision=high)
        moved = scaled_dual + label_sign * solved.reshape(ROWS, CLASSES)
        dual_box = jnp.clip(moved, 0.0, 1.0)
        scaled_dual = moved - dual_box
    return dual_box, scaled_dual
```

```python
import functools

import jax
import jax.numpy as jnp
from jax import lax
from jax.experimental import pallas as pl
from jax.experimental.pallas import tpu as pltpu
from jax.sharding import PartitionSpec as P

CLASSES = 256
ITERS = 2
NN = (((1,), (0,)), ((), ()))
NT = (((1,), (1,)), ((), ()))


def split(x):
    high = x.astype(jnp.bfloat16)
    low = (x - high.astype(jnp.float32)).astype(jnp.bfloat16)
    return high, low


def dot(a, b, dims):
    return lax.dot_general(a, b, dims, preferred_element_type=jnp.float32)


def product(a, b, dims=NN):
    return dot(a[0], b[0], dims) + (dot(a[0], b[1], dims) + dot(a[1], b[0], dims))


def kernel(
    n,
    m,
    labels_ref,
    inverse_hbm,
    basis_hbm,
    solved_hbm,
    capacitance_hbm,
    top_basis_hbm,
    top_solved_hbm,
    top_capacitance_hbm,
    moved_ref,
    inverse_ref,
    basis_ref,
    solved_ref,
    capacitance_ref,
    top_basis_ref,
    top_solved_ref,
    top_capacitance_ref,
    w_out,
    w_in,
    c_all,
    p_out,
    p_in,
    proj,
    t_all,
    in_sem,
    w_send,
    w_recv,
    c_send,
    c_recv,
    p_send,
    p_recv,
    g_send,
    g_recv,
    t_send,
    t_recv,
):
    me = lax.axis_index("leaf")
    grp = lax.axis_index("grp")
    rows = labels_ref.shape[1]
    rank = basis_ref.shape[1]
    top_rank = top_basis_ref.shape[1]
    share = CLASSES // n

    sources = (
        (top_basis_hbm, top_basis_ref),
        (solved_hbm, solved_ref),
        (capacitance_hbm, capacitance_ref),
        (inverse_hbm, inverse_ref),
        (basis_hbm, basis_ref),
        (top_solved_hbm, top_solved_ref),
        (top_capacitance_hbm, top_capacitance_ref),
    )
    loads = [pltpu.make_async_copy(a, b, in_sem.at[i]) for i, (a, b) in enumerate(sources)]
    for load in loads:
        load.start()

    barrier = pltpu.get_barrier_semaphore()
    for d in range(1, n):
        pl.semaphore_signal(
            barrier, inc=1, device_id={"leaf": lax.rem(me + d, n)},
            device_id_type=pl.DeviceIdType.MESH,
        )
    for d in range(1, m):
        pl.semaphore_signal(
            barrier, inc=1, device_id={"grp": lax.rem(grp + d, m)},
            device_id_type=pl.DeviceIdType.MESH,
        )

    def remote(src, dst, send, recv, where):
        return pltpu.make_async_remote_copy(
            src_ref=src, dst_ref=dst, send_sem=send, recv_sem=recv,
            device_id=where, device_id_type=pl.DeviceIdType.MESH,
        )

    sent = []

    loads[0].wait()
    loads[1].wait()
    loads[2].wait()
    top_basis_t = top_basis_ref[...].T
    solved = split(solved_ref[...])
    capacitance = split(capacitance_ref[...])
    coupling = product(split(product(split(top_basis_t), solved)), capacitance)
    for d in range(n):
        w_out[d] = coupling[:, d * rank : (d + 1) * rank]
    pl.semaphore_wait(barrier, n - 1 + m - 1)
    for d in range(1, n):
        dest = lax.rem(me + d, n)
        copy = remote(w_out.at[dest], w_in.at[d], w_send.at[d], w_recv.at[d], {"leaf": dest})
        copy.start()
        sent.append((None, copy))

    pieces = []
    for r in range(rows // 128):
        row = labels_ref[:, r * 128 : (r + 1) * 128].astype(jnp.float32)
        column = jnp.broadcast_to(row, (128, 128)).T
        lanes = lax.broadcasted_iota(jnp.int32, (128, 128), 1)
        pieces.append(
            jnp.concatenate(
                [
                    jnp.where(column == (lanes + k * 128).astype(jnp.float32), 1.0, -1.0)
                    for k in range(CLASSES // 128)
                ],
                axis=1,
            )
        )
    sign = jnp.concatenate(pieces, axis=0)

    loads[3].wait()
    inverse = split(inverse_ref[...])
    exact = sign.astype(jnp.bfloat16)
    local = dot(inverse[0], exact, NN) + dot(inverse[1], exact, NN)

    loads[4].wait()
    loads[5].wait()
    loads[6].wait()
    top_solved = split(top_solved_ref[...])
    top_capacitance = split(top_capacitance_ref[...])
    basis = basis_ref[...]
    w_sum = w_out[me]
    for d in range(1, n):
        remote(w_out.at[0], w_in.at[d], w_send.at[d], w_recv.at[d], {"leaf": me}).wait_recv()
        w_sum = w_sum + w_in[d]
    combined = top_basis_t - product(split(w_sum), split(basis), NT)
    projector = split(jnp.concatenate([basis.T, combined], axis=0))

    scaled_dual = None
    for it in range(ITERS):
        if it:
            rhs = sign * (1.0 + 1.0 * (dual_box - scaled_dual))
            local = product(inverse, split(rhs))
        both = product(projector, split(local))
        p_out[it] = both[rank:, :].T
        for d in range(1, n):
            dest = lax.rem(me + d, n)
            copy = remote(
                p_out.at[it, pl.ds(pl.multiple_of(dest * share, 8), share)],
                p_in.at[it, d], p_send.at[it, d], p_recv.at[it, d], {"leaf": dest},
            )
            copy.start()
            sent.append((None, copy))
        c_all[it, me] = both[:rank, :]

        def step(k, it=it):
            left, right = jnp.maximum(me - k, 0), jnp.minimum(me + k, n - 1)
            has_left, has_right = me - k >= 0, me + k <= n - 1
            for side, src, has, more, dest in (
                (0, left, has_left, me < n - 1, jnp.minimum(me + 1, n - 1)),
                (1, right, has_right, me > 0, jnp.maximum(me - 1, 0)),
            ):
                if k:
                    @pl.when(has)
                    def _(src=src, side=side):
                        remote(
                            c_all.at[it, src], c_all.at[it, src], c_send.at[it, side, k],
                            c_recv.at[it, side, k], {"leaf": me},
                        ).wait_recv()
                if k < n - 1:
                    copy = remote(
                        c_all.at[it, src], c_all.at[it, src], c_send.at[it, side, k],
                        c_recv.at[it, side, k + 1], {"leaf": dest},
                    )

                    @pl.when(has & more)
                    def _(copy=copy):
                        copy.start()

                    sent.append((has & more, copy))

        step(0)

        total = p_out[it, pl.ds(pl.multiple_of(me * share, 8), share)]
        for d in range(1, n):
            remote(
                p_in.at[it, 0], p_in.at[it, d], p_send.at[it, d], p_recv.at[it, d], {"leaf": me}
            ).wait_recv()
            total = total + p_in[it, d]
        proj[it, grp] = total
        for d in range(1, m):
            copy = remote(
                proj.at[it, grp], proj.at[it, grp], g_send.at[it, d], g_recv.at[it, d],
                {"grp": lax.rem(grp + d, m)},
            )
            copy.start()
            sent.append((None, copy))
        step(1)
        for d in range(1, m):
            src = lax.rem(grp + m - d, m)
            remote(
                proj.at[it, src], proj.at[it, src], g_send.at[it, d], g_recv.at[it, d],
                {"grp": grp},
            ).wait_recv()
        stacked = jnp.concatenate([proj[it, g] for g in range(m)], axis=1)
        mine = pl.ds(pl.multiple_of(me * share, 8), share)
        t_all[it, mine] = product(split(stacked), top_capacitance, NT)
        for d in range(1, n):
            copy = remote(
                t_all.at[it, mine], t_all.at[it, mine], t_send.at[it, d], t_recv.at[it, d],
                {"leaf": lax.rem(me + d, n)},
            )
            copy.start()
            sent.append((None, copy))
        for k in range(2, n):
            step(k)
        coeffs = jnp.concatenate([c_all[it, k] for k in range(n)], axis=0)
        group_coef = product(capacitance, split(coeffs))
        inner = local - product(solved, split(group_coef))
        for d in range(1, n):
            src = pl.ds(pl.multiple_of(lax.rem(me + n - d, n) * share, 8), share)
            remote(
                t_all.at[it, src], t_all.at[it, src], t_send.at[it, d], t_recv.at[it, d],
                {"leaf": me},
            ).wait_recv()
        answer = inner - product(top_solved, split(t_all[it]), NT)
        moved = sign * answer
        if it:
            moved = scaled_dual + moved
        if it < ITERS - 1:
            dual_box = jnp.clip(moved, 0.0, 1.0)
            scaled_dual = moved - dual_box
    moved_ref[...] = moved
    for has, copy in sent:
        if has is None:
            copy.wait_send()
        else:
            @pl.when(has)
            def _(copy=copy):
                copy.wait_send()


def shards(
    n,
    m,
    labels,
    leaf_inverse,
    leaf_basis,
    leaf_solved,
    group_capacitance,
    top_basis,
    top_solved,
    top_capacitance,
):
    rows = labels.shape[0]
    rank = leaf_basis.shape[1]
    top_rank = top_basis.shape[1]
    share = CLASSES // n
    arrays = (
        leaf_inverse,
        leaf_basis,
        leaf_solved,
        group_capacitance,
        top_basis,
        top_solved,
        top_capacitance,
    )
    f32 = jnp.float32
    sem = pltpu.SemaphoreType.DMA
    moved = pl.pallas_call(
        functools.partial(kernel, n, m),
        out_shape=jax.ShapeDtypeStruct((rows, CLASSES), f32),
        in_specs=[pl.BlockSpec(memory_space=pltpu.VMEM)]
        + [pl.BlockSpec(memory_space=pl.ANY)] * len(arrays),
        out_specs=pl.BlockSpec(memory_space=pltpu.VMEM),
        scratch_shapes=[pltpu.VMEM(a.shape, f32) for a in arrays]
        + [
            pltpu.VMEM((n, top_rank, rank), f32),
            pltpu.VMEM((n, top_rank, rank), f32),
            pltpu.VMEM((ITERS, n, rank, CLASSES), f32),
            pltpu.VMEM((ITERS, CLASSES, top_rank), f32),
            pltpu.VMEM((ITERS, n, share, top_rank), f32),
            pltpu.VMEM((ITERS, m, share, top_rank), f32),
            pltpu.VMEM((ITERS, CLASSES, top_rank), f32),
            sem((len(arrays),)),
            sem((n,)),
            sem((n,)),
            sem((ITERS, 2, n)),
            sem((ITERS, 2, n)),
            sem((ITERS, n)),
            sem((ITERS, n)),
            sem((ITERS, m)),
            sem((ITERS, m)),
            sem((ITERS, n)),
            sem((ITERS, n)),
        ],
        compiler_params=pltpu.CompilerParams(
            collective_id=0, has_side_effects=True, vmem_limit_bytes=48 * 1024 * 1024
        ),
    )(labels.reshape(1, rows), *arrays)
    dual_box = jnp.clip(moved, 0.0, 1.0)
    return (dual_box, moved - dual_box)


def solution(mesh):
    both = ("grp", "leaf")
    return jax.shard_map(
        functools.partial(shards, mesh.shape["leaf"], mesh.shape["grp"]),
        mesh=mesh,
        in_specs=(P(both),) + (P(both, None),) * 6 + (P("grp", None),),
        out_specs=(P(both, None), P(both, None)),
        check_vma=False,
    )
```

```python
import functools

import jax
import jax.numpy as jnp
from jax import lax
from jax.experimental import pallas as pl
from jax.experimental.pallas import tpu as pltpu
from jax.sharding import PartitionSpec as P

CLASSES = 256
ITERS = 2
CHUNKS = 2
WIDTH = CLASSES // CHUNKS
UNITS = ITERS * CHUNKS
NN = (((1,), (0,)), ((), ()))
NT = (((1,), (1,)), ((), ()))


def split(x):
    high = x.astype(jnp.bfloat16)
    low = (x - high.astype(jnp.float32)).astype(jnp.bfloat16)
    return high, low


def dot(a, b, dims):
    return lax.dot_general(a, b, dims, preferred_element_type=jnp.float32)


def product(a, b, dims=NN):
    return dot(a[0], b[0], dims) + (dot(a[0], b[1], dims) + dot(a[1], b[0], dims))


def kernel(
    n,
    m,
    labels_ref,
    inverse_hbm,
    basis_hbm,
    solved_hbm,
    capacitance_hbm,
    top_basis_hbm,
    top_solved_hbm,
    top_capacitance_hbm,
    moved_ref,
    inverse_ref,
    basis_ref,
    solved_ref,
    capacitance_ref,
    top_basis_ref,
    top_solved_ref,
    top_capacitance_ref,
    w_out,
    w_in,
    c_all,
    p_out,
    p_in,
    proj,
    t_all,
    in_sem,
    w_send,
    w_recv,
    c_send,
    c_recv,
    p_send,
    p_recv,
    g_send,
    g_recv,
    t_send,
    t_recv,
):
    me = lax.axis_index("leaf")
    grp = lax.axis_index("grp")
    rows = labels_ref.shape[1]
    rank = basis_ref.shape[1]
    top_rank = top_basis_ref.shape[1]
    share = WIDTH // n

    sources = (
        (inverse_hbm, inverse_ref),
        (basis_hbm, basis_ref),
        (capacitance_hbm, capacitance_ref),
        (solved_hbm, solved_ref),
        (top_basis_hbm, top_basis_ref),
        (top_solved_hbm, top_solved_ref),
        (top_capacitance_hbm, top_capacitance_ref),
    )
    loads = [pltpu.make_async_copy(a, b, in_sem.at[i]) for i, (a, b) in enumerate(sources)]
    for i in (4, 3, 2, 0, 1, 5, 6):
        loads[i].start()

    barrier = pltpu.get_barrier_semaphore()
    for d in range(1, n):
        pl.semaphore_signal(
            barrier, inc=1, device_id={"leaf": lax.rem(me + d, n)},
            device_id_type=pl.DeviceIdType.MESH,
        )
    for d in range(1, m):
        pl.semaphore_signal(
            barrier, inc=1, device_id={"grp": lax.rem(grp + d, m)},
            device_id_type=pl.DeviceIdType.MESH,
        )

    def remote(src, dst, send, recv, where):
        return pltpu.make_async_remote_copy(
            src_ref=src, dst_ref=dst, send_sem=send, recv_sem=recv,
            device_id=where, device_id_type=pl.DeviceIdType.MESH,
        )

    sent = []

    pieces = []
    for r in range(rows // 128):
        row = labels_ref[:, r * 128 : (r + 1) * 128].astype(jnp.float32)
        column = jnp.broadcast_to(row, (128, 128)).T
        lanes = lax.broadcasted_iota(jnp.int32, (128, 128), 1)
        pieces.append(
            jnp.concatenate(
                [
                    jnp.where(column == (lanes + k * 128).astype(jnp.float32), 1.0, -1.0)
                    for k in range(CLASSES // 128)
                ],
                axis=1,
            )
        )
    sign = jnp.concatenate(pieces, axis=0)

    mine = pl.ds(pl.multiple_of(me * share, 8), share)
    state = [{} for _ in range(UNITS)]

    def begin(u):
        st, chunk = state[u], u % CHUNKS
        st["sign"] = sign[:, chunk * WIDTH : (chunk + 1) * WIDTH]
        if u < CHUNKS:
            exact = st["sign"].astype(jnp.bfloat16)
            st["local"] = dot(inverse[0], exact, NN) + dot(inverse[1], exact, NN)
        else:
            prev = state[u - CHUNKS]
            rhs = st["sign"] * (1.0 + 1.0 * (prev["dual_box"] - prev["scaled_dual"]))
            st["local"] = product(inverse, split(rhs))

    def send_p(u, partial):
        p_out[u] = partial.T
        for d in range(1, n):
            dest = lax.rem(me + d, n)
            copy = remote(
                p_out.at[u, pl.ds(pl.multiple_of(dest * share, 8), share)],
                p_in.at[u, d], p_send.at[u, d], p_recv.at[u, d], {"leaf": dest},
            )
            copy.start()
            sent.append((None, copy))

    def step(u, k):
        left, right = jnp.maximum(me - k, 0), jnp.minimum(me + k, n - 1)
        has_left, has_right = me - k >= 0, me + k <= n - 1
        for side, src, has, more, dest in (
            (0, left, has_left, me < n - 1, jnp.minimum(me + 1, n - 1)),
            (1, right, has_right, me > 0, jnp.maximum(me - 1, 0)),
        ):
            if k:
                @pl.when(has)
                def _(src=src, side=side):
                    remote(
                        c_all.at[u, src], c_all.at[u, src], c_send.at[u, side, k],
                        c_recv.at[u, side, k], {"leaf": me},
                    ).wait_recv()
            if k < n - 1:
                copy = remote(
                    c_all.at[u, src], c_all.at[u, src], c_send.at[u, side, k],
                    c_recv.at[u, side, k + 1], {"leaf": dest},
                )

                @pl.when(has & more)
                def _(copy=copy):
                    copy.start()

                sent.append((has & more, copy))

    def correct(u):
        st = state[u]
        coeffs = jnp.concatenate([c_all[u, k] for k in range(n)], axis=0)
        group_coef = product(capacitance, split(coeffs))
        st["inner"] = st["local"] - product(solved, split(group_coef))

    def gather(u):
        total = p_out[u, mine]
        for d in range(1, n):
            remote(
                p_in.at[u, 0], p_in.at[u, d], p_send.at[u, d], p_recv.at[u, d], {"leaf": me}
            ).wait_recv()
            total = total + p_in[u, d]
        proj[u, grp] = total
        for d in range(1, m):
            copy = remote(
                proj.at[u, grp], proj.at[u, grp], g_send.at[u, d], g_recv.at[u, d],
                {"grp": lax.rem(grp + d, m)},
            )
            copy.start()
            sent.append((None, copy))

    def top(u):
        for d in range(1, m):
            src = lax.rem(grp + m - d, m)
            remote(
                proj.at[u, src], proj.at[u, src], g_send.at[u, d], g_recv.at[u, d], {"grp": grp}
            ).wait_recv()
        stacked = jnp.concatenate([proj[u, g] for g in range(m)], axis=1)
        t_all[u, mine] = product(split(stacked), top_capacitance, NT)
        for d in range(1, n):
            copy = remote(
                t_all.at[u, mine], t_all.at[u, mine], t_send.at[u, d], t_recv.at[u, d],
                {"leaf": lax.rem(me + d, n)},
            )
            copy.start()
            sent.append((None, copy))

    def finish(u):
        st, chunk = state[u], u % CHUNKS
        for d in range(1, n):
            src = pl.ds(pl.multiple_of(lax.rem(me + n - d, n) * share, 8), share)
            remote(
                t_all.at[u, src], t_all.at[u, src], t_send.at[u, d], t_recv.at[u, d], {"leaf": me}
            ).wait_recv()
        moved = st["sign"] * (st["inner"] - product(top_solved, split(t_all[u]), NT))
        if u >= CHUNKS:
            moved = state[u - CHUNKS]["scaled_dual"] + moved
        if u < UNITS - CHUNKS:
            st["dual_box"] = jnp.clip(moved, 0.0, 1.0)
            st["scaled_dual"] = moved - st["dual_box"]
        else:
            moved_ref[:, chunk * WIDTH : (chunk + 1) * WIDTH] = moved

    for i in (2, 3, 4):
        loads[i].wait()
    top_basis_t = top_basis_ref[...].T
    solved = split(solved_ref[...])
    capacitance = split(capacitance_ref[...])
    coupling = product(split(product(split(top_basis_t), solved)), capacitance)
    for d in range(n):
        w_out[d] = coupling[:, d * rank : (d + 1) * rank]
    pl.semaphore_wait(barrier, n - 1 + m - 1)
    for d in range(1, n):
        dest = lax.rem(me + d, n)
        copy = remote(w_out.at[dest], w_in.at[d], w_send.at[d], w_recv.at[d], {"leaf": dest})
        copy.start()
        sent.append((None, copy))
    loads[0].wait()
    inverse = split(inverse_ref[...])
    for u in range(CHUNKS):
        begin(u)
    loads[1].wait()
    loads[5].wait()
    loads[6].wait()
    basis_t = basis_ref[...].T
    top_solved = split(top_solved_ref[...])
    top_capacitance = split(top_capacitance_ref[...])
    w_sum = w_out[me]
    for d in range(1, n):
        remote(w_out.at[0], w_in.at[d], w_send.at[d], w_recv.at[d], {"leaf": me}).wait_recv()
        w_sum = w_sum + w_in[d]
    combined = top_basis_t - product(split(w_sum), split(basis_ref[...]), NT)
    projector = split(jnp.concatenate([basis_t, combined], axis=0))
    for it in range(ITERS):
        units = range(it * CHUNKS, (it + 1) * CHUNKS)
        for u in units:
            if it:
                finish(u - CHUNKS)
                begin(u)
            both = product(projector, split(state[u]["local"]))
            send_p(u, both[rank:, :])
            c_all[u, me] = both[:rank, :]
        for u in units:
            step(u, 0)
        for u in units:
            gather(u)
        for u in units:
            step(u, 1)
        for u in units:
            top(u)
        for k in range(2, n):
            for u in units:
                step(u, k)
        for u in units:
            correct(u)
    for u in range(UNITS - CHUNKS, UNITS):
        finish(u)
    for has, copy in sent:
        if has is None:
            copy.wait_send()
        else:
            @pl.when(has)
            def _(copy=copy):
                copy.wait_send()


def shards(
    n,
    m,
    labels,
    leaf_inverse,
    leaf_basis,
    leaf_solved,
    group_capacitance,
    top_basis,
    top_solved,
    top_capacitance,
):
    rows = labels.shape[0]
    rank = leaf_basis.shape[1]
    top_rank = top_basis.shape[1]
    share = WIDTH // n
    arrays = (
        leaf_inverse,
        leaf_basis,
        leaf_solved,
        group_capacitance,
        top_basis,
        top_solved,
        top_capacitance,
    )
    f32 = jnp.float32
    sem = pltpu.SemaphoreType.DMA
    moved = pl.pallas_call(
        functools.partial(kernel, n, m),
        out_shape=jax.ShapeDtypeStruct((rows, CLASSES), f32),
        in_specs=[pl.BlockSpec(memory_space=pltpu.VMEM)]
        + [pl.BlockSpec(memory_space=pltpu.HBM)] * len(arrays),
        out_specs=pl.BlockSpec(memory_space=pltpu.VMEM),
        scratch_shapes=[pltpu.VMEM(a.shape, f32) for a in arrays]
        + [
            pltpu.VMEM((n, top_rank, rank), f32),
            pltpu.VMEM((n, top_rank, rank), f32),
            pltpu.VMEM((UNITS, n, rank, WIDTH), f32),
            pltpu.VMEM((UNITS, WIDTH, top_rank), f32),
            pltpu.VMEM((UNITS, n, share, top_rank), f32),
            pltpu.VMEM((UNITS, m, share, top_rank), f32),
            pltpu.VMEM((UNITS, WIDTH, top_rank), f32),
            sem((len(arrays),)),
            sem((n,)),
            sem((n,)),
            sem((UNITS, 2, n)),
            sem((UNITS, 2, n)),
            sem((UNITS, n)),
            sem((UNITS, n)),
            sem((UNITS, m)),
            sem((UNITS, m)),
            sem((UNITS, n)),
            sem((UNITS, n)),
        ],
        compiler_params=pltpu.CompilerParams(
            collective_id=0, has_side_effects=True, vmem_limit_bytes=62 * 1024 * 1024
        ),
    )(labels.reshape(1, rows), *arrays)
    dual_box = jnp.clip(moved, 0.0, 1.0)
    return (dual_box, moved - dual_box)


def solution(mesh):
    both = ("grp", "leaf")
    return jax.shard_map(
        functools.partial(shards, mesh.shape["leaf"], mesh.shape["grp"]),
        mesh=mesh,
        in_specs=(P(both),) + (P(both, None),) * 6 + (P("grp", None),),
        out_specs=(P(both, None), P(both, None)),
        check_vma=False,
    )
```
